32 devices in a mesh: pair: 8 (over z, y), aux: 4 (over x, core).
Axes of the slice: x: 2, y: 2, z: 4, core: 2. Of those that a mesh axis runs over, the one named last changes fastest.
Arguments:
- x_panels: float32 [1024, 1024], P(None, 'pair'), may hold values from -0.25 to 0.25
- xbar_panels: float32 [1024, 1024], P(None, 'pair'), may hold values from -6 to 6
- bbar_below: float32 [4096, 1024], P('aux', 'pair'), may hold values from -6 to 6
- l_below: float32 [4096, 1024], P(('aux', 'pair')), may hold values from -0.09375 to 0.09375
- l_cross: float32 [512, 512], P('pair'), may hold values from -0.25 to 0.25
- dinv: float32 [2, 512, 512], P(None, 'pair'), as said below
Outputs:
- bbar_panels: float32 [1024, 1024], P(None, 'pair')
- lbar_below: float32 [4096, 1024], P(('aux', 'pair'))
- lbar_diag: float32 [2, 512, 512], P(None, 'pair')
- lbar_cross: float32 [512, 512], P('pair')
The draws below stay inside these ranges and needn't reach their ends.
Inputs may be any that keep to these rules, and one draw needn't show every extreme that they name: Each dinv[k] is lower triangular with a positive diagonal.
All inputs are finite; a program needn't handle non-finite values.
Results may differ from the reference program's by a relative error of at most 0.00013.
Values sent between devices are 32-bit elements; how exact they have to be, the bound alone decides.
No kernel may reach another device: no remote copies, remote signals or barrier semaphores. Data moves between devices by JAX's collectives and lax.ppermute only.
A program may use at most 64 MiB of HBM per device.

```python
import jax
import jax.numpy as jnp
from jax import lax

NB = 512
PAIRS = 1024
ROWS = 4096


def draw_dinv(key, part):
    first_key, second_key = jax.random.split(jax.random.fold_in(key, 7))
    rows_idx = jnp.arange(NB)[:, None]
    cols_idx = jnp.arange(NB)[None, :]
    lower_mask = (rows_idx > cols_idx).astype(jnp.float32)
    diag_vals = jax.random.uniform(first_key, (2, NB), jnp.float32, 0.5, 2.0)
    spread = 1.0
    lower_vals = jax.random.normal(second_key, (2, NB, NB), jnp.float32) * (spread / jnp.sqrt(1.0 * NB))
    eye_mat = (rows_idx == cols_idx).astype(jnp.float32)
    return lower_vals * lower_mask[None] + diag_vals[:, :, None] * eye_mat[None]


def strengthened(result, key, source, target, parts, factor):
    owner, partner = [(jnp.arange(result.shape[axis_at]) // (result.shape[axis_at] // parts)).reshape([-1 if axis == axis_at else 1 for axis in range(result.ndim)]) for axis_at in (source, target)]
    chosen = jax.random.permutation(key, parts)[partner]
    strong = (owner == chosen) | (owner == (partner + parts // 2) % parts)
    return jnp.where(strong, factor * result, result)


def block_levels(key, dims, cuts, smallest, high):
    def one(axis_at, shards_of):
        heights = jax.random.uniform(jax.random.fold_in(jax.random.fold_in(key, 6), axis_at), (shards_of,), jnp.float32, smallest / len(cuts), high / len(cuts))
        return jnp.repeat(jnp.exp(heights), dims[axis_at] // shards_of).reshape((-1,) + (1,) * (len(dims) - axis_at - 1))

    gain = one(*cuts[0])
    for cut in cuts[1:]:
        gain = gain * one(*cut)
    return gain


def normal_values(rng, dims, scale, most, cuts=(), dtype=jnp.bfloat16):
    factor_of = block_levels(rng, dims, cuts, -0.22, 0.18) if cuts else 1.0
    entries = jax.random.normal(rng, dims, jnp.float32) * scale * factor_of
    return jnp.minimum(jnp.maximum(entries, -most), most).astype(dtype)


def noise_with(own_key, dims, scale, most, cuts, heavy, held_as=jnp.bfloat16):
    entries = scale * jax.random.normal(own_key, dims, jnp.float32)
    if cuts:
        entries = entries * block_levels(own_key, dims, cuts, -0.22, 0.18)
    return jnp.clip(strengthened(entries, jax.random.fold_in(own_key, 3), *heavy), -most, most).astype(held_as)


def setup_inputs(seed: int = 0) -> dict:
    keys = jax.random.split(jax.random.key(seed), 7)
    x_panels = noise_with(keys[0], (2 * NB, PAIRS), PAIRS ** -0.5, 0.25, ((1, 8),), (1, 0, 8, 2.0), jnp.float32)
    xbar_panels = normal_values(keys[1], (2 * NB, PAIRS), 1.0, 6.0, ((1, 8),), jnp.float32)
    bbar_below = noise_with(keys[2], (ROWS, PAIRS), 1.0, 6.0, ((0, 4), (1, 8)), (1, 0, 8, 2.0), jnp.float32)
    l_below = normal_values(keys[3], (ROWS, 2 * NB), ROWS ** -0.5, 0.09375, ((0, 32),), jnp.float32)
    l_cross = normal_values(keys[4], (NB, NB), NB ** -0.5, 0.25, ((0, 8),), jnp.float32)
    dinv = draw_dinv(jax.random.fold_in(keys[6], 71), 0)
    return {"x_panels": x_panels, "xbar_panels": xbar_panels, "bbar_below": bbar_below, "l_below": l_below, "l_cross": l_cross, "dinv": dinv}


def reference(x_panels, xbar_panels, bbar_below, l_below, l_cross, dinv):
    precise = lax.Precision.HIGHEST
    corr = jnp.dot(l_below.T, bbar_below, precision=precise, preferred_element_type=jnp.float32)
    lbar_below = -jnp.dot(bbar_below, x_panels.T, precision=precise, preferred_element_type=jnp.float32)
    bbar_late = jnp.dot(dinv[1].T, xbar_panels[NB:] - corr[NB:], precision=precise, preferred_element_type=jnp.float32)
    cross_term = jnp.dot(l_cross.T, bbar_late, precision=precise, preferred_element_type=jnp.float32)
    bbar_early = jnp.dot(dinv[0].T, xbar_panels[:NB] - corr[:NB] - cross_term, precision=precise, preferred_element_type=jnp.float32)
    x_early = x_panels[:NB]
    x_late = x_panels[NB:]
    diag_early = -jnp.dot(bbar_early, x_early.T, precision=precise, preferred_element_type=jnp.float32)
    diag_late = -jnp.dot(bbar_late, x_late.T, precision=precise, preferred_element_type=jnp.float32)
    lbar_cross = -jnp.dot(bbar_late, x_early.T, precision=precise, preferred_element_type=jnp.float32)
    bbar_panels = jnp.concatenate([bbar_early, bbar_late], axis=0)
    return bbar_panels, lbar_below, jnp.stack([diag_early, diag_late]), lbar_cross
```

```python
import jax
import jax.numpy as jnp
from jax import lax
from jax.sharding import Mesh, PartitionSpec as P

PRECISION = lax.Precision.HIGH
DIRECT_MOST = 8


def fold_with(right_side, pieces):
    return lax.dot_general(
        pieces,
        right_side,
        (((0,), (0,)), ((), ())),
        precision=lax.Precision.HIGHEST,
        preferred_element_type=jnp.float32,
    )


def gathered_body(x_panels, xbar_panels, bbar_below, l_below, l_cross, dinv):
    panel = dinv.shape[2]
    precise = lax.Precision.HIGHEST
    contract_cols = (((1,), (1,)), ((), ()))

    def below_correction(first, count):
        columns = l_below[:, first : first + count]
        folded = fold_with(bbar_below, lax.all_gather(columns, "pair", axis=0, tiled=True))
        return lax.psum(folded, "aux")

    def solve_panel(index, right_side):
        return fold_with(right_side, lax.all_gather(dinv[index], "pair", axis=0, tiled=True))

    lbar_below = lax.psum_scatter(
        -lax.dot_general(
            bbar_below,
            x_panels,
            contract_cols,
            precision=precise,
            preferred_element_type=jnp.float32,
        ),
        "pair",
        scatter_dimension=0,
        tiled=True,
    )
    late_corr = below_correction(panel, panel)
    bbar_late = solve_panel(1, xbar_panels[panel:] - late_corr)
    cross_term = fold_with(bbar_late, lax.all_gather(l_cross, "pair", axis=0, tiled=True))
    early_corr = below_correction(0, panel)
    bbar_early = solve_panel(0, xbar_panels[:panel] - early_corr - cross_term)
    x_early = x_panels[:panel]
    x_late = x_panels[panel:]
    diag_early = -lax.dot_general(
        bbar_early, x_early, contract_cols, precision=precise, preferred_element_type=jnp.float32
    )
    diag_late = -lax.dot_general(
        bbar_late, x_late, contract_cols, precision=precise, preferred_element_type=jnp.float32
    )
    cross_block = -lax.dot_general(
        bbar_late, x_early, contract_cols, precision=precise, preferred_element_type=jnp.float32
    )
    stacked = jnp.stack([diag_early, diag_late, cross_block])
    summed = lax.psum_scatter(stacked, "pair", scatter_dimension=1, tiled=True)
    bbar_panels = jnp.concatenate([bbar_early, bbar_late], axis=0)
    return (bbar_panels, lbar_below, summed[:2], summed[2])


def contract(left, right, left_dims, right_dims):
    return lax.dot_general(
        left,
        right,
        ((left_dims, right_dims), ((), ())),
        precision=PRECISION,
        preferred_element_type=jnp.float32,
    )


def make_body(sizes):
    nz, ny, nx, nc = (sizes[name] for name in ("z", "y", "x", "c"))

    def shift(value, axis, by):
        count = sizes[axis]
        if by % count == 0:
            return value
        return lax.ppermute(value, axis, [(i, (i + by) % count) for i in range(count)])

    def from_ahead(value, axis):
        return jnp.stack([shift(value, axis, -r) for r in range(sizes[axis])])

    def from_behind(value, axis):
        return jnp.stack([shift(value, axis, s) for s in range(sizes[axis])])

    def picked(value, start, count, axis):
        return lax.dynamic_slice_in_dim(value, start, count, axis)

    def body(x_panels, xbar_panels, bbar_below, l_below, l_cross, dinv):
        z, y, x, c = (lax.axis_index(name) for name in ("z", "y", "x", "c"))
        panel = dinv.shape[2]
        cols = x_panels.shape[1]
        q = cols // (nx * nc)
        kk = l_below.shape[0]
        pr = l_cross.shape[0]
        quarter = x * nc + c

        bt = bbar_below.T.reshape(nx, nc, q, nz, ny, kk)
        bt = jnp.roll(bt, (-x, -c, -z, -y), axis=(0, 1, 3, 4))
        blocks = bt.transpose(3, 1, 0, 2, 4, 5).reshape(nz, nc, nx, q, ny * kk)
        bs = jnp.stack([shift(blocks[s], "z", s) for s in range(nz)])

        halves = {"late": panel, "early": 0}

        def corr_of(first):
            columns = l_below[:, first : first + panel]
            lcat = from_ahead(columns, "y").reshape(ny * kk, panel)
            parts = [contract(bs[:, cr], lcat, (3,), (0,)) for cr in range(nc)]
            kept = parts[0]
            for cr in range(1, nc):
                kept = kept + shift(parts[cr], "c", cr)
            total = kept[:, 0]
            for xr in range(1, nx):
                total = total + shift(kept[:, xr], "x", xr)
            out = total[0]
            for s in range(1, nz):
                out = out + shift(total[s], "z", -s)
            return out

        corr_late = corr_of(panel)
        corr_early = corr_of(0)

        xt = picked(x_panels.T, quarter * q, q, 0)
        xbt = picked(xbar_panels.T, quarter * q, q, 0)
        xg = from_ahead(from_ahead(from_behind(xt, "z"), "x"), "c")

        width = panel // nc
        factors = jnp.concatenate([dinv, l_cross[None]])
        piece = picked(factors, c * width, width, 2)
        fg = from_ahead(from_ahead(from_behind(piece, "z"), "y"), "c")
        rows = []
        for z0 in range(nz):
            for y0 in range(ny):
                at = [
                    lax.dynamic_slice(
                        fg,
                        ((c0 - c) % nc, (y0 - y) % ny, (z - z0) % nz, 0, 0, 0),
                        (1, 1, 1, 3, pr, width),
                    ).reshape(3, pr, width)
                    for c0 in range(nc)
                ]
                rows.append(jnp.concatenate(at, axis=2))
        full = jnp.concatenate(rows, axis=1)

        late = contract(xbt[:, panel:] - corr_late, full[1], (1,), (0,))
        cross = contract(late, full[2], (1,), (0,))
        early = contract(xbt[:, :panel] - corr_early - cross, full[0], (1,), (0,))

        below = contract(
            bs.transpose(1, 2, 0, 3, 4).reshape(-1, ny * kk),
            xg.reshape(-1, 2 * panel),
            (0,),
            (0,),
        ).reshape(ny, kk, 2 * panel)
        lbar_below = below[0]
        for yr in range(1, ny):
            lbar_below = lbar_below + shift(below[yr], "y", yr)

        def rows_of(value):
            sent = [
                shift(picked(value, ((z + s) % nz) * (ny * pr), ny * pr, 1), "z", s)
                for s in range(nz)
            ]
            got = from_ahead(from_ahead(jnp.stack(sent), "x"), "c")
            return got.reshape(-1, ny * pr)

        xflat = xg.reshape(-1, 2 * panel)

        def lbar_of(got, first):
            part = contract(got, xflat[:, first : first + panel], (0,), (0,))
            total = picked(part, y * pr, pr, 0)
            for yr in range(1, ny):
                total = total + shift(picked(part, ((y + yr) % ny) * pr, pr, 0), "y", yr)
            return -total

        late_rows = rows_of(late)
        early_rows = rows_of(early)
        diag_late = lbar_of(late_rows, panel)
        lbar_cross = lbar_of(late_rows, 0)
        diag_early = lbar_of(early_rows, 0)

        def all_columns(value):
            got = from_ahead(from_ahead(value, "x"), "c")
            got = jnp.roll(got, (c, x), axis=(0, 1)).transpose(1, 0, 2, 3)
            return got.reshape(cols, panel).T

        bbar_panels = jnp.concatenate([all_columns(early), all_columns(late)])
        return bbar_panels, -lbar_below, jnp.stack([diag_early, diag_late]), lbar_cross

    return body


def solution(mesh):
    pairs, auxes = mesh.shape["pair"], mesh.shape["aux"]
    ny = 2 if pairs % 2 == 0 else 1
    nc = 2 if auxes % 2 == 0 else 1
    sizes = {"z": pairs // ny, "y": ny, "x": auxes // nc, "c": nc}
    direct = max(sizes.values()) <= DIRECT_MOST
    if direct:
        mesh = Mesh(mesh.devices.reshape(tuple(sizes.values())), tuple(sizes))
    pair, aux = (("z", "y"), ("x", "c")) if direct else (("pair",), ("aux",))
    in_specs = (
        P(None, pair),
        P(None, pair),
        P(aux, pair),
        P(aux + pair, None),
        P(pair, None),
        P(None, pair, None),
    )
    out_specs = (P(None, pair), P(aux + pair, None), P(None, pair, None), P(pair, None))
    body = make_body(sizes) if direct else gathered_body
    return jax.shard_map(
        body, mesh=mesh, in_specs=in_specs, out_specs=out_specs, check_vma=False
    )
```
